32 devices in a mesh: dom: 32 (over z, y, x, core).
Axes of the slice: x: 2, y: 2, z: 4, core: 2. Of those that a mesh axis runs over, the one named last changes fastest.
Arguments:
- elem_state: bfloat16 [1024, 5, 216], P('dom'), may hold values from -6 to 6
- mass_inverse: bfloat16 [1024, 216, 216], P('dom'), as said below
- jacobian: bfloat16 [1024, 216, 216], P('dom'), may hold values from -0.4375 to 0.4375
- elem_order: int32 [1024], P('dom'), may hold values from 2 to 5
- new_owner: int32 [1024], P('dom'), may hold values from 0 to 31, as said below
- neighbors: int32 [1024, 6], P('dom'), may hold values from -1 to 1023, as said below
- penalty: bfloat16 [1024, 6], P('dom'), may hold values from 0.049804688 to 0.5
- closure_in: bfloat16 [64, 5], replicated, may hold values from -2.5 to 2.5
- closure_out: bfloat16 [5, 64], replicated, may hold values from -0.75 to 0.75
Outputs:
- migrated: float32 [1536, 5, 216], P('dom')
- migrated_mass: bfloat16 [1536, 216, 216], P('dom')
- migrated_jacobian: bfloat16 [1536, 216, 216], P('dom')
The draws below stay inside these ranges and needn't reach their ends.
Inputs may be any that keep to these rules, and one draw needn't show every extreme that they name: new_owner never falls along the elements; each element's new owner is the device that holds it before the repartition (32 elements a device, in order) or a device beside that one; at most 8 elements pass from one device to each neighbour, and each device owns between 16 and 48 elements afterwards; 8 and 48 are reached. `neighbors`: each entry is -1 or an element within 16 places of its own element along the curve; the distance 16 is reached. `mass_inverse`: each tile has a diagonal of order one and small off-diagonal entries.
All inputs are finite; a program needn't handle non-finite values.
Results may differ from the reference program's by a relative error of at most 0.01.
Values may be sent and summed in bfloat16 or wider, within the bound.
No kernel may reach another device: no remote copies, remote signals or barrier semaphores. Data moves between devices by JAX's collectives and lax.ppermute only.
A program may use at most 128 MiB of HBM per device.

```python
import math
import jax
import jax.numpy as jnp
from jax import lax

NODE = 216
VARS = 5
HID = 64
FACES = 6
SWEEPS = 2
E_DEV = 32
MOVE = 8
CAP = 48
REACH = 16
ELEMS = 1024
N_DOM = 32


def draw_mass_inverse(key, part):
    first_key, second_key = jax.random.split(jax.random.fold_in(key, 11))
    node_ids = jnp.arange(NODE)
    diagonal = jax.random.uniform(first_key, (ELEMS, NODE), jnp.float32, 0.6, 1.6)
    spread = jax.random.normal(second_key, (ELEMS, NODE, NODE), jnp.float32) * (0.6 / NODE ** 0.5)
    spread = spread.at[:, node_ids, node_ids].set(diagonal)
    return spread.astype(jnp.bfloat16)


def draw_new_owner(key, part):
    device_count = ELEMS // E_DEV
    device_ids = jnp.arange(device_count + 1, dtype=jnp.int32)
    shifts = jax.random.randint(jax.random.fold_in(key, 23), (device_count + 1,), -MOVE, MOVE + 1)
    shifts = jnp.where(device_ids == 1, -MOVE, shifts)
    shifts = jnp.where(device_ids == 2, MOVE, shifts)
    shifts = jnp.where((device_ids == 0) | (device_ids == device_count), 0, shifts)
    cuts = device_ids * E_DEV + shifts
    element_ids = jnp.arange(ELEMS, dtype=jnp.int32)
    inner = cuts[1:device_count]
    owners = jnp.sum((element_ids[:, None] >= inner[None, :]).astype(jnp.int32), axis=1)
    return owners.astype(jnp.int32)


def draw_neighbors(key, part):
    first_key, second_key = jax.random.split(jax.random.fold_in(key, 37))
    distance = jax.random.randint(first_key, (ELEMS, 6), 1, REACH + 1)
    direction = 2 * jax.random.randint(second_key, (ELEMS, 6), 0, 2) - 1
    element_ids = jnp.arange(ELEMS, dtype=jnp.int32)[:, None]
    targets = element_ids + distance * direction
    targets = targets.at[REACH, 0].set(0)
    targets = targets.at[ELEMS - 1 - REACH, 1].set(ELEMS - 1)
    targets = targets.at[0, 2].set(-1)
    targets = jnp.where((targets < 0) | (targets >= ELEMS), -1, targets)
    return targets.astype(jnp.int32)


def place_ends(drawn, stream_key, low, largest):
    place = [jax.random.randint(jax.random.fold_in(stream_key, axis), (), 0, length) for axis, length in enumerate(drawn.shape)]
    widest = drawn.shape.index(max(drawn.shape))
    beside = place[:widest] + [(place[widest] + 1) % drawn.shape[widest]] + place[widest + 1:]
    return drawn.at[tuple(place)].set(low).at[tuple(beside)].set(largest)


def block_levels(key, extent, cuts, least, top_value):
    gain, own = 1.0, jax.random.fold_in(key, 6)
    for dim, parts in cuts:
        steps = jnp.exp(jax.random.uniform(jax.random.fold_in(own, dim), (parts,), jnp.float32, least / len(cuts), top_value / len(cuts)))
        gain = gain * jnp.repeat(steps, extent[dim] // parts).reshape([-1 if axis == dim else 1 for axis in range(len(extent))])
    return gain


def noise(key, shape, scale, bound, cuts=(), kind=jnp.bfloat16):
    result = scale * jax.random.normal(key, shape, jnp.float32)
    if cuts:
        result = result * block_levels(key, shape, cuts, -0.22, 0.18)
    return jnp.clip(result, -bound, bound).astype(kind)


def setup_inputs(seed: int = 0) -> dict:
    key_of = jax.random.split(jax.random.key(seed), 10)
    elem_state = noise(key_of[0], (ELEMS, VARS, NODE), 1.0, 6.0, ((0, 32),))
    mass_inverse = draw_mass_inverse(jax.random.fold_in(key_of[9], 71), 0)
    jacobian = noise(key_of[2], (ELEMS, NODE, NODE), NODE ** -0.5, 0.4375, ((0, 32),))
    elem_order = place_ends(jax.random.randint(key_of[3], (ELEMS,), 2, 6), jax.random.fold_in(key_of[3], 1), 2, 5).astype(jnp.int32)
    new_owner = draw_new_owner(jax.random.fold_in(key_of[9], 71), 0)
    neighbors = draw_neighbors(jax.random.fold_in(key_of[9], 71), 0)
    penalty = jnp.clip(jnp.exp(math.log(0.5) - 2.306499 * jax.random.uniform(key_of[6], (ELEMS, FACES), jnp.float32) ** block_levels(key_of[6], (ELEMS, FACES), ((0, 32),), -0.2, 0.2)), 0.049804688, 0.5).astype(jnp.bfloat16)
    closure_in = noise(key_of[7], (HID, VARS), VARS ** -0.5, 2.5)
    closure_out = noise(key_of[8], (VARS, HID), HID ** -0.5, 0.75)
    return dict(elem_state=elem_state, mass_inverse=mass_inverse, jacobian=jacobian, elem_order=elem_order, new_owner=new_owner, neighbors=neighbors, penalty=penalty, closure_in=closure_in, closure_out=closure_out)


def keep_mask(order_rows, node_count):
    limit = (order_rows + 1) ** 3
    node_ids = jnp.arange(node_count, dtype=jnp.int32)
    return (node_ids[None, :] < limit[:, None]).astype(jnp.float32)[:, None, :]


def reference(elem_state, mass_inverse, jacobian, elem_order, new_owner, neighbors, penalty, closure_in, closure_out):
    retained = keep_mask(elem_order, NODE)
    current = elem_state.astype(jnp.float32)
    mass_blocks = mass_inverse.reshape(N_DOM, E_DEV, NODE, NODE)
    jac_blocks = jacobian.reshape(N_DOM, E_DEV, NODE, NODE)
    near_ids = jnp.where(neighbors < 0, ELEMS, neighbors).astype(jnp.int32)
    for sweep_idx in range(SWEEPS):
        rounded = current.astype(jnp.bfloat16)

        def apply_mass(pair):
            tiles, values = pair
            return jnp.einsum('enm,evm->evn', tiles.astype(jnp.float32), values.astype(jnp.float32),
                              precision=lax.Precision.HIGHEST).astype(jnp.bfloat16)

        weighted = lax.map(apply_mass, (mass_blocks, rounded.reshape(N_DOM, E_DEV, VARS, NODE)))
        weighted = weighted.reshape(ELEMS, VARS, NODE)
        padded = jnp.concatenate([weighted, jnp.zeros((1, VARS, NODE), jnp.bfloat16)], axis=0)

        def update(group):
            tiles, own, near_idx, weights_face, values, prior, mask_rows = group
            beside = padded[near_idx]
            difference = beside.astype(jnp.float32) - own.astype(jnp.float32)[:, None]
            coupling = jnp.sum(weights_face.astype(jnp.float32)[:, :, None, None] * difference, axis=1)
            transport = jnp.einsum('enm,evn->evm', tiles.astype(jnp.float32), own.astype(jnp.float32),
                                   precision=lax.Precision.HIGHEST)
            hidden = jnp.tanh(jnp.einsum('hv,evn->ehn', closure_in.astype(jnp.float32), values.astype(jnp.float32),
                                         precision=lax.Precision.HIGHEST)).astype(jnp.bfloat16)
            closure = jnp.einsum('vh,ehn->evn', closure_out.astype(jnp.float32), hidden.astype(jnp.float32),
                                 precision=lax.Precision.HIGHEST)
            return (prior + transport + coupling + closure) * mask_rows

        current = lax.map(update, (jac_blocks,
                                   weighted.reshape(N_DOM, E_DEV, VARS, NODE),
                                   near_ids.reshape(N_DOM, E_DEV, FACES),
                                   penalty.reshape(N_DOM, E_DEV, FACES),
                                   rounded.reshape(N_DOM, E_DEV, VARS, NODE),
                                   current.reshape(N_DOM, E_DEV, VARS, NODE),
                                   retained.reshape(N_DOM, E_DEV, 1, NODE)))
        current = current.reshape(ELEMS, VARS, NODE)
    device_ids = jnp.arange(N_DOM, dtype=jnp.int32)
    counts = jnp.sum((new_owner[None, :] == device_ids[:, None]).astype(jnp.int32), axis=1)
    starts = jnp.cumsum(counts) - counts
    slots = jnp.arange(ELEMS, dtype=jnp.int32) - starts[new_owner]
    target_rows = (new_owner * CAP + slots).astype(jnp.int32)
    migrated = jnp.zeros((N_DOM * CAP, VARS, NODE), jnp.float32).at[target_rows].set(current)
    migrated_mass = jnp.zeros((N_DOM * CAP, NODE, NODE), jnp.bfloat16).at[target_rows].set(mass_inverse)
    migrated_jacobian = jnp.zeros((N_DOM * CAP, NODE, NODE), jnp.bfloat16).at[target_rows].set(jacobian)
    return (migrated, migrated_mass, migrated_jacobian)
```

```python
import functools

import jax
import jax.numpy as jnp
from jax import lax
from jax.experimental import pallas as pl
from jax.experimental.pallas import tpu as pltpu
from jax.sharding import PartitionSpec as P

SUB = 8
LANE = 128
BF = jnp.bfloat16
F32 = jnp.float32

ANY = pl.BlockSpec(memory_space=pltpu.MemorySpace.HBM)
VM = pl.BlockSpec(memory_space=pltpu.VMEM)
SM = pl.BlockSpec(memory_space=pltpu.SMEM)
GROUP = 4


def cross_pairs(size):
    return [p for i in range(1, size - 1, 2) for p in ((i, i + 1), (i + 1, i))]


def intra_pairs(size):
    return [p for i in range(0, size - 1, 2) for p in ((i, i + 1), (i + 1, i))]


def swap_cross(x):
    return lax.ppermute(x, "dom", cross_pairs(lax.axis_size("dom")))


def swap_intra(x):
    return lax.ppermute(x, "dom", intra_pairs(lax.axis_size("dom")))


def lanes(shape):
    return lax.broadcasted_iota(jnp.int32, shape, len(shape) - 1)


def group_blocks(node):
    rem = node - LANE
    return GROUP + -(-GROUP * rem // LANE)


def pack_group(tile, put, node):
    rem = node - LANE
    rolled = []
    for k in range(GROUP):
        t = tile(k)
        put(k, t[:, :LANE])
        wide = jnp.concatenate(
            [t[:, LANE:].astype(F32), jnp.zeros((node, LANE - rem), F32)], axis=1
        )
        shift = k * rem % LANE
        rolled.append(pltpu.roll(wide, shift, 1) if shift else wide)
    lane = lanes((node, LANE))
    for b in range(group_blocks(node) - GROUP):
        block = None
        for k in range(GROUP):
            low, high = k * rem - b * LANE, (k + 1) * rem - b * LANE
            if high <= 0 or low >= LANE:
                continue
            block = rolled[k] if block is None else jnp.where(lane >= low, rolled[k], block)
        put(GROUP + b, block.astype(BF))


def unpack_group(block, put, node):
    rem = node - LANE
    lane = lanes((node, LANE))
    extra = [block(GROUP + b).astype(F32) for b in range(group_blocks(node) - GROUP)]
    for k in range(GROUP):
        first, last = k * rem // LANE, ((k + 1) * rem - 1) // LANE
        wide = extra[first]
        if last != first:
            wide = jnp.where(lane >= k * rem - first * LANE, wide, extra[last])
        shift = k * rem % LANE
        if shift:
            wide = pltpu.roll(wide, LANE - shift, 1)
        put(k, block(k), wide[:, :rem].astype(BF))


def tile_pass(values, wait, tiles, contract):
    nvar, count, node = values.shape
    rows = nvar * SUB
    member = lax.broadcasted_iota(jnp.int32, (rows, node), 0) % SUB
    outs = []
    for g in range(count // SUB):
        wait(g)
        part = values[:, g * SUB : (g + 1) * SUB, :].reshape(rows, node)
        acc = jnp.zeros((rows, node), F32)
        for k in range(SUB):
            lhs = jnp.where(member == k, part, 0.0).astype(BF)
            acc = acc + lax.dot_general(
                lhs,
                tiles[g * SUB + k],
                (((1,), (contract,)), ((), ())),
                preferred_element_type=F32,
            )
        outs.append(acc.reshape(nvar, SUB, node))
    return jnp.concatenate(outs, axis=1)


def spread_nets(cin, cout):
    hid, nvar = cin.shape

    def grow(matrix, rows, cols):
        left = (
            lax.broadcasted_iota(jnp.int32, (rows * SUB, rows), 0) // SUB
            == lax.broadcasted_iota(jnp.int32, (rows * SUB, rows), 1)
        ).astype(BF)
        right = (
            lax.broadcasted_iota(jnp.int32, (cols, cols * SUB), 1) // SUB
            == lax.broadcasted_iota(jnp.int32, (cols, cols * SUB), 0)
        ).astype(BF)
        tall = jnp.dot(left, matrix, preferred_element_type=F32).astype(BF)
        full = jnp.dot(tall, right, preferred_element_type=F32)
        shape = (rows * SUB, cols * SUB)
        same = (
            lax.broadcasted_iota(jnp.int32, shape, 0) % SUB
            == lax.broadcasted_iota(jnp.int32, shape, 1) % SUB
        )
        return jnp.where(same, full, 0.0).astype(BF)

    return grow(cin, hid, nvar), grow(cout, nvar, hid)


def closure_pass(values, net_in, net_out):
    nvar, count, node = values.shape
    outs = []
    for g in range(count // SUB):
        part = values[:, g * SUB : (g + 1) * SUB, :].reshape(nvar * SUB, node).astype(BF)
        hidden = jnp.tanh(jnp.dot(net_in, part, preferred_element_type=F32)).astype(BF)
        out = jnp.dot(net_out, hidden, preferred_element_type=F32)
        outs.append(out.reshape(nvar, SUB, node))
    return jnp.concatenate(outs, axis=1)


def couple(both, ext):
    half = both.shape[0] // 2
    out = jnp.dot(both, ext, preferred_element_type=F32)
    return out[:half] + out[half:]


def loader(src, dst, sems, step):
    count = src.shape[0] // step

    def copy(g):
        return pltpu.make_async_copy(
            src.at[pl.ds(g * step, step)], dst.at[pl.ds(g * step, step)], sems.at[g]
        )

    def start():
        for g in range(count):
            copy(g).start()

    return start, lambda g: copy(g).wait()


def pack_first(mass, out, tiles, sem, *, moving):
    node = mass.shape[1]
    parity = lax.axis_index("dom") % 2
    first = parity * (mass.shape[0] - moving)
    copy = pltpu.make_async_copy(mass.at[pl.ds(first, GROUP)], tiles, sem)
    copy.start()
    copy.wait()

    def put(b, value):
        out[b] = value

    pack_group(lambda k: tiles[k], put, node)


def pack_rest(mass, jac, mid, last, intra, tiles, own, sems, sends, *, moving):
    node, count = mass.shape[1], mass.shape[0]
    parity = lax.axis_index("dom") % 2
    first = parity * (count - moving)
    other = (1 - parity) * (count - moving)
    loads = [
        pltpu.make_async_copy(mass.at[pl.ds(first + GROUP, GROUP)], tiles.at[0], sems.at[0]),
        pltpu.make_async_copy(jac.at[pl.ds(first, GROUP)], tiles.at[1], sems.at[1]),
        pltpu.make_async_copy(jac.at[pl.ds(first + GROUP, GROUP)], tiles.at[2], sems.at[2]),
        pltpu.make_async_copy(mass.at[pl.ds(other, moving)], own.at[0], sems.at[3]),
        pltpu.make_async_copy(jac.at[pl.ds(other, moving)], own.at[1], sems.at[4]),
    ]
    for load in loads:
        load.start()
    blocks = group_blocks(node)
    for i in range(3):
        loads[i].wait()
        ref, base = (mid, i * blocks) if i < 2 else (last, 0)

        def put(b, value, ref=ref, base=base):
            ref[base + b] = value

        pack_group(lambda k, i=i: tiles[i, k], put, node)
        if i < 2:
            loads[3 + i].wait()
            pltpu.make_async_copy(
                own.at[i], intra.at[pl.ds(i * moving, moving)], sends.at[i]
            ).start()
    for i in range(2):
        pltpu.make_async_copy(
            own.at[i], intra.at[pl.ds(i * moving, moving)], sends.at[i]
        ).wait()


def column(row, count):
    shape = (count, count)
    same = lax.broadcasted_iota(jnp.int32, shape, 0) == lanes(shape)
    return jnp.sum(jnp.where(same, row, 0.0), axis=1, keepdims=True)


def store_sides(left, right, xout, iout):
    even = lax.axis_index("dom") % 2 == 0

    @pl.when(even)
    def _():
        for low, value in left:
            xout[low : low + value.shape[0], :] = value
        for low, value in right:
            iout[low : low + value.shape[0], :] = value

    @pl.when(jnp.logical_not(even))
    def _():
        for low, value in left:
            iout[low : low + value.shape[0], :] = value
        for low, value in right:
            xout[low : low + value.shape[0], :] = value


def first_mass(
    state, mass, near, penalty, order, owner,
    wout, both_out, keep_out, xout, iout,
    tiles, sems, *, reach,
):
    nvar, count, node = state.shape
    position = lax.axis_index("dom")
    start, wait = loader(mass, tiles, sems, SUB)
    start()
    faces = near.shape[0]
    found = near[...]
    located = jnp.where(found < 0, -1, found - (position * count - reach))
    pen = penalty[...].astype(F32)
    row = lax.broadcasted_iota(jnp.int32, (node, count), 0)
    col = lanes((node, count))
    matrix = jnp.zeros((node, count), F32)
    total = jnp.zeros((1, count), F32)
    for f in range(faces):
        matrix = matrix + jnp.where(row == located[f : f + 1], pen[f : f + 1], 0.0)
        total = total + pen[f : f + 1]
    matrix = matrix - jnp.where(row == col + reach, total, 0.0)
    matrix = matrix.T
    high = matrix.astype(BF)
    low = (matrix - high.astype(F32)).astype(BF)
    both_out[0:count, :] = high
    both_out[count : 2 * count, :] = low
    edge = order[...] + 1
    limit = column((edge * edge * edge).astype(F32), count)
    lane = lanes((count, node))
    keep_out[...] = (lane.astype(F32) < limit).astype(F32)
    goes = [column((owner[...] == position + d).astype(F32), count) for d in (-1, 1)]
    meta = [jnp.where(lane < LANE, limit, g).astype(BF) for g in goes]

    weighted = tile_pass(state[...].astype(F32), wait, tiles, 1).astype(BF)
    wout[...] = weighted
    sides = []
    for s, lo in enumerate((0, count - reach)):
        hi = lo + reach
        parts = [(v * reach, weighted[v, lo:hi, :]) for v in range(nvar)]
        base = nvar * reach
        parts += [(base, high[lo:hi]), (base + reach, low[lo:hi]), (base + 2 * reach, meta[s][lo:hi])]
        sides.append(parts)
    store_sides(sides[0], sides[1], xout, iout)


def first_rest(state, weighted, both, jac, cin, cout, part, nin, nout, tiles, sems, *, reach):
    nvar, count, node = state.shape
    start, wait = loader(jac, tiles, sems, SUB)
    start()
    net_in, net_out = spread_nets(cin[...], cout[...])
    nin[...] = net_in
    nout[...] = net_out
    values = state[...].astype(F32)
    local = weighted[...]
    pad = jnp.zeros((reach, node), BF)
    span = count + 2 * reach
    weights = both[:, :span]
    own = jnp.stack(
        [couple(weights, jnp.concatenate([pad, local[v], pad], axis=0)) for v in range(nvar)]
    )
    total = values + own + closure_pass(values, net_in, net_out)
    part[...] = total + tile_pass(local.astype(F32), wait, tiles, 0)


def take_sides(xin, iin, left, right):
    even = lax.axis_index("dom") % 2 == 0

    @pl.when(even)
    def _():
        left[...] = xin[...]
        right[...] = iin[...]

    @pl.when(jnp.logical_not(even))
    def _():
        left[...] = iin[...]
        right[...] = xin[...]


def halo_term(weights, left, right, nvar, reach, count, node):
    gap = jnp.zeros((count, node), BF)
    return jnp.stack(
        [
            couple(
                weights,
                jnp.concatenate(
                    [
                        left[v * reach : (v + 1) * reach, :],
                        gap,
                        right[v * reach : (v + 1) * reach, :],
                    ],
                    axis=0,
                ),
            )
            for v in range(nvar)
        ]
    )


def second(
    xin, iin, part, both, keep, nin, nout, mass, jac,
    wout, pout, xout, iout,
    mtiles, jtiles, left, right, msems, jsems, *, reach, moving,
):
    nvar, count, node = part.shape
    mstart, mwait = loader(mass, mtiles, msems, SUB)
    jstart, jwait = loader(jac, jtiles, jsems, SUB)
    mstart()
    jstart()
    take_sides(xin, iin, left, right)
    weights = both[:, : count + 2 * reach]
    current = part[...] + halo_term(weights, left, right, nvar, reach, count, node)
    current = current * keep[...][None]
    rounded = current.astype(BF).astype(F32)
    weighted = tile_pass(rounded, mwait, mtiles, 1).astype(BF)
    wout[...] = weighted
    pad = jnp.zeros((reach, node), BF)
    own = jnp.stack(
        [couple(weights, jnp.concatenate([pad, weighted[v], pad], axis=0)) for v in range(nvar)]
    )
    total = current + own + closure_pass(rounded, nin[...], nout[...])
    total = total + tile_pass(weighted.astype(F32), jwait, jtiles, 0)
    pout[...] = total
    sides = []
    for lo, edge in ((0, 0), (count - reach, count - moving)):
        parts = [(v * reach, weighted[v, lo : lo + reach, :]) for v in range(nvar)]
        near = total[:, edge : edge + moving, :].reshape(nvar * moving, node).astype(BF)
        parts.append((nvar * reach, near))
        sides.append(parts)
    store_sides(sides[0], sides[1], xout, iout)


def counts_of(owner, left, right, meta, reach):
    position = lax.axis_index("dom")
    below, kept = jnp.int32(0), jnp.int32(0)
    for e in range(owner.shape[0]):
        below = below + (owner[e] < position).astype(jnp.int32)
        kept = kept + (owner[e] == position).astype(jnp.int32)

    def taken(ref):
        flags = ref[meta : meta + reach, :].astype(F32)
        flags = jnp.where(lanes(flags.shape) == LANE, flags, 0.0)
        return jnp.sum(flags).astype(jnp.int32)

    return taken(left), below, kept, taken(right)


def place_own(
    xin1, iin1, owner, mass, jac,
    mout, jout, cnt_out,
    mtiles, jtiles, zero, left, right, msems, jsems, osems, zsems, *, reach, meta,
):
    count = mass.shape[0]
    slots = mout.shape[0]
    mstart, mwait = loader(mass, mtiles, msems, SUB)
    jstart, jwait = loader(jac, jtiles, jsems, SUB)
    mstart()
    jstart()
    take_sides(xin1, iin1, left, right)
    before, below, kept, after = counts_of(owner, left, right, meta, reach)
    cnt_out[0] = before
    cnt_out[1] = below
    cnt_out[2] = kept
    cnt_out[3] = after
    zero[...] = jnp.zeros_like(zero)
    filled = before + kept + after

    def blank(s):
        return (
            pltpu.make_async_copy(zero, mout.at[s], zsems.at[0, s]),
            pltpu.make_async_copy(zero, jout.at[s], zsems.at[1, s]),
        )

    def mass_copy(e):
        return pltpu.make_async_copy(mtiles.at[e], mout.at[before + e - below], osems.at[0, e])

    def jac_copy(e):
        return pltpu.make_async_copy(jtiles.at[e], jout.at[before + e - below], osems.at[1, e])

    def each(low, high, fun):
        lax.fori_loop(low, high, lambda i, c: (fun(i), c)[1], 0)

    def start_blank(s):
        for copy in blank(s):
            copy.start()

    def wait_all(copies):
        for copy in copies:
            copy.wait()

    each(filled, slots, start_blank)
    for g in range(count // SUB):
        mwait(g)
    each(below, below + kept, lambda e: mass_copy(e).start())
    for g in range(count // SUB):
        jwait(g)
    each(below, below + kept, lambda e: jac_copy(e).start())
    each(filled, slots, lambda s: wait_all(blank(s)))
    each(below, below + kept, lambda e: wait_all((mass_copy(e), jac_copy(e))))


def finish_state(
    xin1, iin1, xin2, iin2, part, weighted, both, keep, owner,
    out, left1, right1, left2, right2, joined, *, reach, moving, meta,
):
    nvar, count, node = part.shape
    slots = out.shape[1]
    take_sides(xin1, iin1, left1, right1)
    take_sides(xin2, iin2, left2, right2)
    before, below, kept, after = counts_of(owner, left1, right1, meta, reach)
    weights = both[:, : count + 2 * reach]
    span = count + 2 * reach
    current = part[...] + halo_term(weights, left2, right2, nvar, reach, count, node)
    joined[:, moving : moving + count, :] = current * keep[...][None]
    base = nvar * reach
    lane = lanes((moving, node)).astype(F32)
    blank = jnp.zeros((span - reach, node), BF)
    local = weighted[...]
    for ref1, ref2, pick, at, near in (
        (left1, left2, reach - moving, 0, 0),
        (right1, right2, 0, moving + count, 1),
    ):
        both_side = jnp.concatenate(
            [
                ref1[base : base + reach, :span].astype(F32)[pick : pick + moving],
                ref1[base + reach : base + 2 * reach, :span].astype(F32)[pick : pick + moving],
            ],
            axis=0,
        ).astype(BF)
        limit = ref1[meta : meta + reach, :LANE].astype(F32)[pick : pick + moving, 0:1]
        stay = (lane < limit).astype(F32)
        partial = ref2[base : base + nvar * moving, :].astype(F32)
        for v in range(nvar):
            if near == 0:
                ext = jnp.concatenate([blank, local[v, :reach, :]], axis=0)
            else:
                ext = jnp.concatenate([local[v, count - reach :, :], blank], axis=0)
            value = partial[v * moving : (v + 1) * moving] + couple(both_side, ext)
            joined[v, at : at + moving, :] = value * stay
    lead = moving - before + below
    filled = before + kept + after
    turn = lax.rem(slots - lead, slots)
    live = lax.broadcasted_iota(jnp.int32, (slots, node), 0) < filled
    for v in range(nvar):
        out[v] = jnp.where(live, pltpu.roll(joined[v], turn, 0), 0.0)


def place_early(cnt, c0, c1, intra, min_, jin, mout, jout, blocks, tiles, near, sems, osems, isems, *, moving):
    del min_, jin
    node = tiles.shape[2]
    size = group_blocks(node)
    even = lax.axis_index("dom") % 2 == 0
    loads = [
        pltpu.make_async_copy(c0, blocks.at[pl.ds(0, size)], sems.at[0]),
        pltpu.make_async_copy(c1, blocks.at[pl.ds(size, 2 * size)], sems.at[1]),
        pltpu.make_async_copy(intra, near, sems.at[2]),
    ]
    for load in loads:
        load.start()
    before, kept, after = cnt[0], cnt[2], cnt[3]
    left_slot, right_slot = before - moving, before + kept
    x_low = jnp.where(even, moving - before, 0)
    x_high = jnp.where(even, moving, after)
    x_slot = jnp.where(even, left_slot, right_slot)
    i_low = jnp.where(even, 0, moving - before)
    i_high = jnp.where(even, after, moving)
    i_slot = jnp.where(even, right_slot, left_slot)

    def each(low, high, fun):
        lax.fori_loop(low, high, lambda i, c: (fun(i), c)[1], 0)

    def from_near(k):
        return (
            pltpu.make_async_copy(near.at[k], mout.at[i_slot + k], isems.at[0, k]),
            pltpu.make_async_copy(near.at[moving + k], jout.at[i_slot + k], isems.at[1, k]),
        )

    def start_near(k):
        for copy in from_near(k):
            copy.start()

    def wait_near(k):
        for copy in from_near(k):
            copy.wait()

    loads[2].wait()
    each(i_low, i_high, start_near)

    def unpack(g):
        def put(k, main, rest):
            tiles[g * GROUP + k, :, :LANE] = main
            tiles[g * GROUP + k, :, LANE:] = rest

        unpack_group(lambda b: blocks[g * size + b], put, node)

    loads[0].wait()
    unpack(0)
    loads[1].wait()
    unpack(1)

    def mass_copy(k):
        return pltpu.make_async_copy(tiles.at[k], mout.at[x_slot + k], osems.at[k])

    each(x_low, x_high, lambda k: mass_copy(k).start())
    unpack(2)

    def jac_copy(k):
        return pltpu.make_async_copy(tiles.at[moving + k], jout.at[x_slot + k], osems.at[moving + k])

    top = jnp.minimum(x_high, GROUP)
    each(x_low, top, lambda k: jac_copy(k).start())
    each(i_low, i_high, wait_near)
    each(x_low, x_high, lambda k: mass_copy(k).wait())
    each(x_low, top, lambda k: jac_copy(k).wait())


def place_last(cnt, c2, jin, jout, tiles, osems, *, moving):
    del jin
    node = tiles.shape[2]
    even = lax.axis_index("dom") % 2 == 0
    before, kept, after = cnt[0], cnt[2], cnt[3]
    low = jnp.where(even, moving - before, 0)
    high = jnp.where(even, moving, after)
    slot = jnp.where(even, before - moving, before + kept)

    def put(k, main, rest):
        tiles[k, :, :LANE] = main
        tiles[k, :, LANE:] = rest

    unpack_group(lambda b: c2[b], put, node)

    def copy(k):
        return pltpu.make_async_copy(tiles.at[k - GROUP], jout.at[slot + k], osems.at[k])

    def each(fun):
        lax.fori_loop(jnp.maximum(low, GROUP), high, lambda i, c: (fun(i), c)[1], 0)

    each(lambda k: copy(k).start())
    each(lambda k: copy(k).wait())


def cost(flops, moved):
    return pl.CostEstimate(flops=flops, bytes_accessed=moved, transcendentals=0)


def call(kernel, outs, ins, specs, out_specs, scratch, aliases=None, moved=4_000_000):
    return pl.pallas_call(
        kernel,
        out_shape=outs,
        in_specs=specs,
        out_specs=out_specs,
        scratch_shapes=scratch,
        input_output_aliases=aliases or {},
        cost_estimate=cost(1_000_000, moved),
        compiler_params=pltpu.CompilerParams(vmem_limit_bytes=40 * 1024 * 1024),
    )(*ins)


def shards(
    elem_state, mass_inverse, jacobian, elem_order, new_owner, neighbors, penalty, closure_in, closure_out
):
    count, nvar, node = elem_state.shape
    hid = closure_in.shape[0]
    moving, reach = count // 4, count // 2
    slots = count + 2 * moving
    size = group_blocks(node)
    meta = nvar * reach + 2 * reach
    rows1 = meta + reach
    rows2 = nvar * (reach + moving)
    sds = jax.ShapeDtypeStruct
    dma = pltpu.SemaphoreType.DMA
    tile_buf = pltpu.VMEM((count, node, node), BF)
    gsems = dma((count // SUB,))

    state = jnp.transpose(elem_state, (1, 0, 2))
    near, pen = neighbors.T, penalty.T
    order, owner = elem_order[None, :], new_owner[None, :]

    c0 = call(
        functools.partial(pack_first, moving=moving),
        sds((size, node, LANE), BF), (mass_inverse,), [ANY], VM,
        [pltpu.VMEM((GROUP, node, node), BF), dma],
        moved=1_000_000,
    )
    r0 = swap_cross(c0)

    weighted, both, keep, x1, i1 = call(
        functools.partial(first_mass, reach=reach),
        (sds((nvar, count, node), BF), sds((2 * count, node), BF), sds((count, node), F32),
         sds((rows1, node), BF), sds((rows1, node), BF)),
        (state, mass_inverse, near, pen, order, owner),
        [VM, ANY, VM, VM, VM, VM], (VM,) * 5,
        [tile_buf, gsems],
    )
    rx1 = swap_cross(x1)
    ri1 = swap_intra(i1)

    c1, c2, ci = call(
        functools.partial(pack_rest, moving=moving),
        (sds((2 * size, node, LANE), BF), sds((size, node, LANE), BF), sds((2 * moving, node, node), BF)),
        (mass_inverse, jacobian), [ANY, ANY], (VM, VM, ANY),
        [pltpu.VMEM((3, GROUP, node, node), BF), pltpu.VMEM((2, moving, node, node), BF), dma((5,)), dma((2,))],
    )
    r1 = swap_cross(c1)
    rci = swap_intra(ci)

    part, nin, nout = call(
        functools.partial(first_rest, reach=reach),
        (sds((nvar, count, node), F32), sds((hid * SUB, nvar * SUB), BF), sds((nvar * SUB, hid * SUB), BF)),
        (state, weighted, both, jacobian, closure_in, closure_out),
        [VM, VM, VM, ANY, VM, VM], (VM, VM, VM),
        [tile_buf, gsems],
    )

    side1 = pltpu.VMEM((rows1, node), BF)
    side2 = pltpu.VMEM((rows2, node), BF)
    weighted2, part2, x2, i2 = call(
        functools.partial(second, reach=reach, moving=moving),
        (sds((nvar, count, node), BF), sds((nvar, count, node), F32),
         sds((rows2, node), BF), sds((rows2, node), BF)),
        (rx1, ri1, part, both, keep, nin, nout, mass_inverse, jacobian),
        [VM] * 7 + [ANY, ANY], (VM,) * 4,
        [tile_buf, tile_buf, side1, side1, gsems, gsems], moved=8_000_000,
    )
    rx2 = swap_cross(x2)
    ri2 = swap_intra(i2)
    r2 = swap_cross(c2)

    big = sds((slots, node, node), BF)
    mout, jout, cnt = call(
        functools.partial(place_own, reach=reach, meta=meta),
        (big, big, sds((4,), jnp.int32)),
        (rx1, ri1, new_owner, mass_inverse, jacobian),
        [VM, VM, SM, ANY, ANY], (ANY, ANY, SM),
        [tile_buf, tile_buf, pltpu.VMEM((node, node), BF), side1, side1, gsems, gsems,
         dma((2, count)), dma((2, slots))],
        moved=16_000_000,
    )
    final = call(
        functools.partial(finish_state, reach=reach, moving=moving, meta=meta),
        sds((nvar, slots, node), F32),
        (rx1, ri1, rx2, ri2, part2, weighted2, both, keep, new_owner),
        [VM] * 8 + [SM], VM,
        [side1, side1, side2, side2, pltpu.VMEM((nvar, slots, node), F32)],
        moved=2_000_000,
    )
    mout, jout = call(
        functools.partial(place_early, moving=moving),
        (big, big),
        (cnt, r0, r1, rci, mout, jout),
        [SM] + [ANY] * 5, (ANY, ANY),
        [pltpu.VMEM((3 * size, node, LANE), BF), pltpu.VMEM((3 * GROUP, node, node), BF),
         pltpu.VMEM((2 * moving, node, node), BF), dma((3,)), dma((2 * moving,)), dma((2, moving))],
        aliases={4: 0, 5: 1}, moved=6_000_000,
    )
    jout = call(
        functools.partial(place_last, moving=moving),
        big, (cnt, r2, jout), [SM, VM, ANY], ANY,
        [pltpu.VMEM((GROUP, node, node), BF), dma((moving,))],
        aliases={2: 0}, moved=1_000_000,
    )
    return jnp.transpose(final, (1, 0, 2)), mout, jout


def solution(mesh):
    placed = (
        P("dom", None, None),
        P("dom", None, None),
        P("dom", None, None),
        P("dom"),
        P("dom"),
        P("dom", None),
        P("dom", None),
        P(),
        P(),
    )

    return jax.shard_map(
        shards,
        mesh=mesh,
        in_specs=placed,
        out_specs=(P("dom", None, None), P("dom", None, None), P("dom", None, None)),
        check_vma=False,
    )
```
